32 devices in a mesh: scenes: 2 (over x), rows: 16 (over z, y, core).
Axes of the slice: x: 2, y: 2, z: 4, core: 2. Of those that a mesh axis runs over, the one named last changes fastest.
Arguments:
- images: float32 [64, 128, 128], P(('scenes', 'rows')), parts along dimension 0, may hold values from -6 to 6
- conv_weight: float32 [3, 3, 128, 128], replicated, may hold values from -0.1875 to 0.1875
- lift_weight: float32 [320, 128], replicated, may hold values from -0.5 to 0.5
- vol_weight: float32 [3, 3, 3, 32, 40], replicated, may hold values from -0.1875 to 0.1875
Outputs:
- filtered: float32 [64, 32, 48, 128], P(('scenes', 'rows')), parts along dimension 0
The draws below stay inside these ranges and needn't reach their ends.
There are 2 independent parts, one for each index of `scenes`. The reference program is written for one: setup_inputs(seed, part) draws one part's arguments, and reference() takes and returns one part's arrays. A program takes and returns all parts, laid end to end along the dimension named above; an argument that names none is the same for every part. Nothing has to cross between parts.
All inputs are finite; a program needn't handle non-finite values.
Results may differ from the reference program's by a relative error of at most 0.0001.
Values sent between devices are 32-bit elements; how exact they have to be, the bound alone decides.
A program may use at most 128 MiB of HBM per device.

```python
import jax
import jax.numpy as jnp
from jax import lax

CIN = 128
FEAT = 320
GROUPS = 40
DISP = 48
OUTC = 32
COLS = 128
HEIGHT = 16


def block_scale(stream_key, dims, pieces, least, largest):
    factor_of = 1.0
    for position, blocks in pieces:
        heights = jax.random.uniform(jax.random.fold_in(jax.random.fold_in(stream_key, 6), position), (blocks,), jnp.float32, least / len(pieces), largest / len(pieces))
        factor_of = factor_of * jnp.repeat(jnp.exp(heights), dims[position] // blocks).reshape((-1,) + (1,) * (len(dims) - 1 - position))
    return factor_of


def centred(rng, shape, spread, most, split=(), dtype=jnp.bfloat16):
    factor_of = block_scale(rng, shape, split, -0.22, 0.18) if split else 1.0
    array = jax.random.normal(rng, shape, jnp.float32) * spread * factor_of
    return jnp.minimum(jnp.maximum(array, -most), most).astype(dtype)


def setup_inputs(seed: int = 0, part: int = 0) -> dict:
    seeds = jax.random.split(jax.random.key(seed), 5)
    own_keys = jax.random.split(jax.random.fold_in(seeds[4], part), 5)
    return {
        "images": centred(own_keys[0], (2 * HEIGHT, CIN, COLS), 1.0, 6.0, ((0, 16),), jnp.float32),
        "conv_weight": centred(seeds[1], (3, 3, CIN, CIN), (9 * CIN) ** -0.5, 0.1875, (), jnp.float32),
        "lift_weight": centred(seeds[2], (FEAT, CIN), CIN ** -0.5, 0.5, (), jnp.float32),
        "vol_weight": centred(seeds[3], (3, 3, 3, OUTC, GROUPS), (27 * GROUPS) ** -0.5, 0.1875, (), jnp.float32),
    }


precise = lax.Precision.HIGHEST


def conv_plane(planes, weight, padding):
    result = lax.conv_general_dilated(planes[None], weight, (1, 1), padding, dimension_numbers=("NHCW", "HWOI", "NHCW"), precision=precise)
    return result[0]


def lift_features(weight, hidden):
    return jnp.einsum("fi,ric->rfc", weight, hidden, precision=precise)


def correlate(anchor, other, groups, disparities):
    row_count, channels, columns = anchor.shape
    padded = jnp.pad(other, ((0, 0), (0, 0), (disparities, 0)))
    layers = []
    for offset in range(disparities):
        shifted = padded[:, :, disparities - offset:disparities - offset + columns]
        product = (anchor * shifted).reshape(row_count, groups, channels // groups, columns)
        layers.append(jnp.mean(product, axis=2))
    return jnp.stack(layers, axis=2)


def conv_volume(volume, weight, padding):
    result = lax.conv_general_dilated(volume[None], weight, (1, 1, 1), padding, dimension_numbers=("NHCDW", "HDWOI", "NHCDW"), precision=precise)
    return result[0]


def reference(images, conv_weight, lift_weight, vol_weight):
    middle = images.shape[0] // 2
    offset_rows = middle // 2
    unrolled = jnp.roll(images, -offset_rows, axis=0)
    left_feat = lift_features(lift_weight, jax.nn.relu(conv_plane(unrolled[:middle], conv_weight, ((1, 1), (1, 1)))))
    right_feat = lift_features(lift_weight, jax.nn.relu(conv_plane(unrolled[middle:], conv_weight, ((1, 1), (1, 1)))))
    left_cost = correlate(left_feat, right_feat, GROUPS, DISP)
    right_cost = jnp.flip(correlate(jnp.flip(right_feat, -1), jnp.flip(left_feat, -1), GROUPS, DISP), -1)
    padding = ((1, 1), (1, 1), (1, 1))
    joined = jnp.concatenate([conv_volume(left_cost, vol_weight, padding), conv_volume(right_cost, vol_weight, padding)], axis=0)
    return jnp.roll(joined, offset_rows, axis=0)
```

```python
import functools

import jax
import jax.numpy as jnp
from jax import lax
from jax.experimental import pallas as pl
from jax.experimental.pallas import tpu as pltpu
from jax.sharding import PartitionSpec as P

DISP = 48
LANES = 128
f32, bf16 = jnp.float32, jnp.bfloat16


def split(x):
    hi = x.astype(bf16)
    return hi, (x - hi.astype(f32)).astype(bf16)


def dot(a, b):
    return jnp.dot(a, b, preferred_element_type=f32)


def dot3(stacked, rows, hi, lo):
    both = dot(stacked, hi)
    return both[:rows] + both[rows:] + dot(stacked[:rows], lo)


def taps(y, size, lane):
    cols = y.shape[1]
    before = jnp.where(lane >= 1, pltpu.roll(y[:size], 1, 1), 0.0)
    after = jnp.where(lane < cols - 1, pltpu.roll(y[2 * size :], cols - 1, 1), 0.0)
    return y[size : 2 * size] + before + after


def compute(own, other, cw, lw, vw, out, feat_a, feat_b, cost_hi, cost_lo, vol_f, vol_2):
    position = lax.axis_index("rows")
    devices = lax.axis_size("rows")
    quarter = devices // 4
    starts = (position == quarter) | (position == 3 * quarter)
    ends = (position == quarter - 1) | (position == 3 * quarter - 1)
    is_right = (position < quarter) | (position >= 3 * quarter)

    framed, cin, cols = own.shape
    rows = framed - 4
    halo = rows + 2
    feat = lw.shape[0]
    outc, groups = vw.shape[3:]
    per = feat // groups
    depth = halo * groups
    used = 3 * depth
    padded = vol_f.shape[1]
    lane = lax.broadcasted_iota(jnp.int32, (1, cols), 1)

    vol_f[...] = jnp.zeros_like(vol_f)
    for dd in range(3):
        for dc in range(3):
            for r in range(rows):
                for dr in range(3):
                    top = (dc * rows + r) * outc
                    left = dd * depth + (r + dr) * groups
                    vol_f[top : top + outc, left : left + groups] = vw[dr, dd, dc] * (1.0 / per)
    high, low = split(vol_f[...])
    m = 3 * rows * outc
    vol_2[:m] = high
    vol_2[m:] = low

    wide = jnp.concatenate([cw[dr].reshape(3 * cin, cin) for dr in range(3)], axis=1)
    conv_2 = jnp.concatenate(split(wide), axis=0)
    lift = jnp.concatenate([lw[pl.ds(k, groups, stride=per), :] for k in range(per)], axis=0)
    lift_2 = jnp.concatenate(split(lift), axis=0)
    parts = []
    for s in range(framed):
        x = jnp.concatenate([own[s], other[s]], axis=1)
        if s < 2:
            x = jnp.where(starts, 0.0, x)
        if s >= rows + 2:
            x = jnp.where(ends, 0.0, x)
        parts.append(split(x))
    for r in range(halo):
        hi = jnp.concatenate([parts[r + k][0] for k in range(3)], axis=0)
        lo = jnp.concatenate([parts[r + k][1] for k in range(3)], axis=0)
        y = dot3(conv_2, 3 * cin, hi, lo)
        here = jnp.maximum(taps(y[:, :cols], cin, lane), 0.0)
        there = jnp.maximum(taps(y[:, cols:], cin, lane), 0.0)
        if r == 0:
            here = jnp.where(starts, 0.0, here)
        if r == halo - 1:
            here = jnp.where(ends, 0.0, here)
        f = dot3(lift_2, feat, *split(jnp.concatenate([here, there], axis=1)))
        for k in range(per):
            feat_a[k, r * groups : (r + 1) * groups, :] = f[k * groups : (k + 1) * groups, :cols]
            feat_b[k, r * groups : (r + 1) * groups, :] = f[k * groups : (k + 1) * groups, cols:]

    for buf in (cost_hi, cost_lo):
        buf[:depth] = jnp.zeros((depth, cols), bf16)
        tail = buf.shape[0] - (DISP + 1) * depth
        buf[(DISP + 1) * depth :] = jnp.zeros((tail, cols), bf16)
    reach = jnp.where(is_right, cols - 1 - lane, lane)

    @pl.loop(0, depth // 16)
    def _(j):
        base = pl.multiple_of(j * 16, 16)
        a = [feat_a[k, pl.ds(base, 16), :] for k in range(per)]
        b = [feat_b[k, pl.ds(base, 16), :] for k in range(per)]

        def at(d, carry):
            shift = jnp.where(is_right, lax.rem(cols - d, cols), d)
            total = a[0] * pltpu.roll(b[0], shift, 1)
            for k in range(1, per):
                total += a[k] * pltpu.roll(b[k], shift, 1)
            hi, lo = split(jnp.where(reach >= d, total, 0.0))
            place = pl.ds(pl.multiple_of((d + 1) * depth + base, 16), 16)
            cost_hi[place, :] = hi
            cost_lo[place, :] = lo
            return carry

        lax.fori_loop(0, DISP, at, 0, unroll=4)

    @pl.loop(0, DISP // 2)
    def _(pair):
        d = pair * 2
        first = pl.ds(pl.multiple_of(d * depth, 16), padded)
        second = pl.ds(pl.multiple_of((d + 1) * depth, 16), padded)
        hi = jnp.concatenate([cost_hi[first, :], cost_hi[second, :]], axis=1)
        lo = jnp.concatenate([cost_lo[first, :], cost_lo[second, :]], axis=1)
        y = dot3(vol_2[...], m, hi, lo)
        for h in range(2):
            z = taps(y[:, h * cols : (h + 1) * cols], rows * outc, lane)
            out[pl.ds(d + h, rows * outc, stride=DISP), :] = z


def shifted(x, by):
    size = lax.axis_size("rows")
    return lax.ppermute(x, "rows", [(i, (i + by) % size) for i in range(size)])


def framed(x):
    return jnp.concatenate([shifted(x[-2:], 1), x, shifted(x[:2], -1)], axis=0)


def on_device(images, conv_weight, lift_weight, vol_weight):
    rows, _, cols = images.shape
    outc, groups = vol_weight.shape[3:]
    per = lift_weight.shape[0] // groups
    depth = (rows + 2) * groups
    padded = -(-3 * depth // 256) * 256
    m = 3 * rows * outc
    length = (DISP + 1) * depth - 2 * depth + padded + depth
    own = framed(images)
    other = framed(shifted(images, lax.axis_size("rows") // 2))
    vmem = pl.BlockSpec(memory_space=pltpu.VMEM)
    flat = pl.pallas_call(
        compute,
        out_shape=jax.ShapeDtypeStruct((rows * outc * DISP, cols), f32),
        in_specs=[vmem] * 5,
        out_specs=vmem,
        scratch_shapes=[
            pltpu.VMEM((per, depth, cols), f32),
            pltpu.VMEM((per, depth, cols), f32),
            pltpu.VMEM((length, cols), bf16),
            pltpu.VMEM((length, cols), bf16),
            pltpu.VMEM((m, padded), f32),
            pltpu.VMEM((2 * m, padded), bf16),
        ],
        compiler_params=pltpu.CompilerParams(vmem_limit_bytes=48 << 20),
    )(own, other, conv_weight, lift_weight, vol_weight)
    return flat.reshape(rows, outc, DISP, cols)


def solution(mesh):
    placed = (P(("scenes", "rows"), None, None), P(), P(), P())
    return jax.shard_map(
        on_device,
        mesh=mesh,
        in_specs=placed,
        out_specs=P(("scenes", "rows"), None, None, None),
        check_vma=False,
    )
```

```python
import functools

import jax
import jax.numpy as jnp
from jax import lax
from jax.experimental import pallas as pl
from jax.experimental.pallas import tpu as pltpu
from jax.sharding import PartitionSpec as P

DISP = 48
CHUNK = 4
LANES = 128
f32, bf16 = jnp.float32, jnp.bfloat16


def split(x):
    hi = x.astype(bf16)
    return hi, (x - hi.astype(f32)).astype(bf16)


def dot(a, b):
    return jnp.dot(a, b, preferred_element_type=f32)


def dot3(stacked, rows, hi, lo):
    both = dot(stacked, hi)
    return both[:rows] + both[rows:] + dot(stacked[:rows], lo)


def taps(y, size, lane):
    cols = y.shape[1]
    before = jnp.where(lane >= 1, pltpu.roll(y[:size], 1, 1), 0.0)
    after = jnp.where(lane < cols - 1, pltpu.roll(y[2 * size :], cols - 1, 1), 0.0)
    return y[size : 2 * size] + before + after


def compute(own, other, cw, lw, vw, out, feat_a, feat_b, cost_hi, cost_lo, vol_f, vol_2):
    position = lax.axis_index("rows")
    devices = lax.axis_size("rows")
    quarter = devices // 4
    starts = (position == quarter) | (position == 3 * quarter)
    ends = (position == quarter - 1) | (position == 3 * quarter - 1)
    is_right = (position < quarter) | (position >= 3 * quarter)

    framed, cin, cols = own.shape
    rows = framed - 4
    halo = rows + 2
    feat = lw.shape[0]
    outc, groups = vw.shape[3:]
    per = feat // groups
    depth = halo * groups
    used = 3 * depth
    padded = vol_f.shape[1]
    lane = lax.broadcasted_iota(jnp.int32, (1, cols), 1)

    vol_f[...] = jnp.zeros_like(vol_f)
    for dd in range(3):
        for dc in range(3):
            for r in range(rows):
                for dr in range(3):
                    top = (dc * rows + r) * outc
                    left = dd * depth + (r + dr) * groups
                    vol_f[top : top + outc, left : left + groups] = vw[dr, dd, dc] * (1.0 / per)
    high, low = split(vol_f[...])
    m = 3 * rows * outc
    vol_2[:m] = high
    vol_2[m:] = low

    wide = jnp.concatenate([cw[dr].reshape(3 * cin, cin) for dr in range(3)], axis=1)
    conv_2 = jnp.concatenate(split(wide), axis=0)
    lift = jnp.concatenate([lw[pl.ds(k, groups, stride=per), :] for k in range(per)], axis=0)
    lift_2 = jnp.concatenate(split(lift), axis=0)
    parts = []
    for s in range(framed):
        x = jnp.concatenate([own[s], other[s]], axis=1)
        if s < 2:
            x = jnp.where(starts, 0.0, x)
        if s >= rows + 2:
            x = jnp.where(ends, 0.0, x)
        parts.append(split(x))
    for r in range(halo):
        hi = jnp.concatenate([parts[r + k][0] for k in range(3)], axis=0)
        lo = jnp.concatenate([parts[r + k][1] for k in range(3)], axis=0)
        y = dot3(conv_2, 3 * cin, hi, lo)
        here = jnp.maximum(taps(y[:, :cols], cin, lane), 0.0)
        there = jnp.maximum(taps(y[:, cols:], cin, lane), 0.0)
        if r == 0:
            here = jnp.where(starts, 0.0, here)
        if r == halo - 1:
            here = jnp.where(ends, 0.0, here)
        f = dot3(lift_2, feat, *split(jnp.concatenate([here, there], axis=1)))
        for k in range(per):
            feat_a[k, r * groups : (r + 1) * groups, :] = f[k * groups : (k + 1) * groups, :cols]
            feat_b[k, r * groups : (r + 1) * groups, :] = f[k * groups : (k + 1) * groups, cols:]

    for buf in (cost_hi, cost_lo):
        buf[:depth] = jnp.zeros((depth, cols), bf16)
        tail = buf.shape[0] - (DISP + 1) * depth
        buf[(DISP + 1) * depth :] = jnp.zeros((tail, cols), bf16)
    reach = jnp.where(is_right, cols - 1 - lane, lane)

    def correlate(disparities):
        shifts = [jnp.where(is_right, (cols - d) % cols, d) for d in disparities]
        for base in range(0, depth, 16):
            a = [feat_a[k, base : base + 16, :] for k in range(per)]
            b = [feat_b[k, base : base + 16, :] for k in range(per)]
            for d, shift in zip(disparities, shifts):
                total = a[0] * pltpu.roll(b[0], shift, 1)
                for k in range(1, per):
                    total += a[k] * pltpu.roll(b[k], shift, 1)
                hi, lo = split(jnp.where(reach >= d, total, 0.0))
                place = (d + 1) * depth + base
                cost_hi[place : place + 16, :] = hi
                cost_lo[place : place + 16, :] = lo

    def filtered(d):
        first, second = d * depth, (d + 1) * depth
        hi, lo = [
            jnp.concatenate([buf[first : first + padded, :], buf[second : second + padded, :]], axis=1)
            for buf in (cost_hi, cost_lo)
        ]
        y = dot3(vol_2[...], m, hi, lo)
        for h in range(2):
            z = taps(y[:, h * cols : (h + 1) * cols], rows * outc, lane)
            out[pl.ds(d + h, rows * outc, stride=DISP), :] = z

    correlate(range(CHUNK + 2))
    for d in range(0, DISP, CHUNK):
        correlate(range(d + CHUNK + 2, min(d + 2 * CHUNK + 2, DISP)))
        for e in range(d, d + CHUNK, 2):
            filtered(e)


def shifted(x, by):
    size = lax.axis_size("rows")
    return lax.ppermute(x, "rows", [(i, (i + by) % size) for i in range(size)])


def framed(x):
    return jnp.concatenate([shifted(x[-2:], 1), x, shifted(x[:2], -1)], axis=0)


def on_device(images, conv_weight, lift_weight, vol_weight):
    rows, _, cols = images.shape
    outc, groups = vol_weight.shape[3:]
    per = lift_weight.shape[0] // groups
    depth = (rows + 2) * groups
    padded = -(-3 * depth // 256) * 256
    m = 3 * rows * outc
    length = (DISP + 1) * depth - 2 * depth + padded + depth
    own = framed(images)
    other = framed(shifted(images, lax.axis_size("rows") // 2))
    vmem = pl.BlockSpec(memory_space=pltpu.VMEM)
    flat = pl.pallas_call(
        compute,
        out_shape=jax.ShapeDtypeStruct((rows * outc * DISP, cols), f32),
        in_specs=[vmem] * 5,
        out_specs=vmem,
        scratch_shapes=[
            pltpu.VMEM((per, depth, cols), f32),
            pltpu.VMEM((per, depth, cols), f32),
            pltpu.VMEM((length, cols), bf16),
            pltpu.VMEM((length, cols), bf16),
            pltpu.VMEM((m, padded), f32),
            pltpu.VMEM((2 * m, padded), bf16),
        ],
        compiler_params=pltpu.CompilerParams(vmem_limit_bytes=48 << 20),
    )(own, other, conv_weight, lift_weight, vol_weight)
    return flat.reshape(rows, outc, DISP, cols)


def solution(mesh):
    placed = (P(("scenes", "rows"), None, None), P(), P(), P())
    return jax.shard_map(
        on_device,
        mesh=mesh,
        in_specs=placed,
        out_specs=P(("scenes", "rows"), None, None, None),
        check_vma=False,
    )
```

```python
import jax
import jax.numpy as jnp
from jax import lax
from jax.experimental import pallas as pl
from jax.experimental.pallas import tpu as pltpu
from jax.sharding import PartitionSpec as P

DISP = 48
CHUNK = 4
STEP = 8
MESH = pl.DeviceIdType.MESH
f32, bf16 = jnp.float32, jnp.bfloat16


def split(x):
    hi = x.astype(bf16)
    return hi, (x - hi.astype(f32)).astype(bf16)


def dot(a, b):
    return jnp.dot(a, b, preferred_element_type=f32)


def dot3(stacked, rows, hi, lo):
    both = dot(stacked, hi)
    return both[:rows] + both[rows:] + dot(stacked[:rows], lo)


def taps(y, size, lane):
    cols = y.shape[1]
    before = jnp.where(lane >= 1, pltpu.roll(y[:size], 1, 1), 0.0)
    after = jnp.where(lane < cols - 1, pltpu.roll(y[2 * size :], cols - 1, 1), 0.0)
    return y[size : 2 * size] + before + after


def place_of():
    position = lax.axis_index("rows")
    quarter = lax.axis_size("rows") // 4
    starts = (position == quarter) | (position == 3 * quarter)
    ends = (position == quarter - 1) | (position == 3 * quarter - 1)
    is_right = (position < quarter) | (position >= 3 * quarter)
    return starts, ends, is_right


def gather(
    images, cw, lw, vw, feat_a, feat_b, vol_2,
    before, after, there, there_before, there_after, vol_f, conv_2, lift_2, send, recv,
):
    me, size = lax.axis_index("rows"), lax.axis_size("rows")
    up, down, partner = [lax.rem(me + by, size) for by in (1, size - 1, size // 2)]
    starts, ends, _ = place_of()
    rows, cin, cols = images.shape
    halo = rows + 2
    feat = lw.shape[0]
    outc, groups = vw.shape[3:]
    per = feat // groups
    depth = halo * groups
    lane = lax.broadcasted_iota(jnp.int32, (1, cols), 1)

    barrier = pltpu.get_barrier_semaphore()
    for to in (up, down, partner):
        pl.semaphore_signal(barrier, inc=1, device_id={"rows": to}, device_id_type=MESH)
    pl.semaphore_wait(barrier, 3)

    def copy(n, source, target, to):
        return pltpu.make_async_remote_copy(
            src_ref=source,
            dst_ref=target,
            send_sem=send.at[n],
            recv_sem=recv.at[n],
            device_id={"rows": to},
            device_id_type=MESH,
        )

    last, first = pl.ds(rows - 2, 2), pl.ds(0, 2)
    across = copy(0, images, there, partner)
    near = [copy(1, images.at[last], before, up), copy(2, images.at[first], after, down)]
    relays = [copy(3, there.at[last], there_before, up), copy(4, there.at[first], there_after, down)]
    across.start()
    for one in near:
        one.start()

    vol_f[...] = jnp.zeros_like(vol_f)
    for dd in range(3):
        for dc in range(3):
            for r in range(rows):
                for dr in range(3):
                    top = (dc * rows + r) * outc
                    left = dd * depth + (r + dr) * groups
                    vol_f[top : top + outc, left : left + groups] = vw[dr, dd, dc] * (1.0 / per)
    m = 3 * rows * outc
    vol_2[:m], vol_2[m:] = split(vol_f[...])
    wide = jnp.concatenate([cw[dr].reshape(3 * cin, cin) for dr in range(3)], axis=1)
    conv_2[: 3 * cin], conv_2[3 * cin :] = split(wide)
    lift = jnp.concatenate([lw[pl.ds(k, groups, stride=per), :] for k in range(per)], axis=0)
    lift_2[:feat], lift_2[feat:] = split(lift)

    def features(above, middle, below, result, cut):
        parts = []
        for s in range(rows + 4):
            if s < 2:
                x = jnp.where(starts, 0.0, above[s])
            elif s < rows + 2:
                x = middle[s - 2]
            else:
                x = jnp.where(ends, 0.0, below[s - 2 - rows])
            parts.append(split(x))
        for r in range(0, halo, 2):
            pair = (r, min(r + 1, halo - 1))
            hi, lo = [
                jnp.concatenate(
                    [jnp.concatenate([parts[t + k][i] for k in range(3)], axis=0) for t in pair], axis=1
                )
                for i in range(2)
            ]
            y = dot3(conv_2[...], 3 * cin, hi, lo)
            hidden = []
            for n, t in enumerate(pair):
                h = jnp.maximum(taps(y[:, n * cols : (n + 1) * cols], cin, lane), 0.0)
                if cut and t == 0:
                    h = jnp.where(starts, 0.0, h)
                if cut and t == halo - 1:
                    h = jnp.where(ends, 0.0, h)
                hidden.append(h)
            f = dot3(lift_2[...], feat, *split(jnp.concatenate(hidden, axis=1)))
            for n, t in enumerate(pair):
                for k in range(per):
                    part = f[k * groups : (k + 1) * groups, n * cols : (n + 1) * cols]
                    result[k, t * groups : (t + 1) * groups, :] = part

    for one in near:
        one.wait_recv()
    features(before, images, after, feat_a, True)
    across.wait_recv()
    for one in relays:
        one.start()
    for one in relays:
        one.wait_recv()
    features(there_before, there, there_after, feat_b, False)
    for one in (across, *near, *relays):
        one.wait_send()


def compute(first_a, first_b, vol_2, out, feat_a, feat_b, cost_hi, cost_lo):
    _, _, is_right = place_of()
    per, depth, cols = first_a.shape
    m, padded = vol_2.shape
    m = m // 2
    lane = lax.broadcasted_iota(jnp.int32, (1, cols), 1)

    for buf in (cost_hi, cost_lo):
        buf[:depth] = jnp.zeros((depth, cols), bf16)
        tail = buf.shape[0] - (DISP + 1) * depth
        buf[(DISP + 1) * depth :] = jnp.zeros((tail, cols), bf16)
    reach = jnp.where(is_right, cols - 1 - lane, lane)

    def turned(x, by):
        cut = by % cols
        return x if cut == 0 else pltpu.roll(x, jnp.where(is_right, cols - cut, cut), 1)

    def correlate(disparities):
        for base in range(0, depth, 16):
            at = slice(base, base + 16)
            for d in disparities:
                step, b = divmod(d, STEP)
                total = None
                for k in range(per):
                    if b == 0 and step > 0:
                        feat_a[step, k, at, :] = turned(first_a[k, at, :], -STEP * step)
                    if step == 0 and b > 0:
                        feat_b[b, k, at, :] = turned(first_b[k, at, :], b)
                    left = feat_a[step, k, at, :] if step else first_a[k, at, :]
                    term = left * (feat_b[b, k, at, :] if b else first_b[k, at, :])
                    total = term if total is None else total + term
                hi, lo = split(jnp.where(reach >= d, turned(total, STEP * step), 0.0))
                place = (d + 1) * depth + base
                cost_hi[place : place + 16, :] = hi
                cost_lo[place : place + 16, :] = lo

    def filtered(d):
        first, second = d * depth, (d + 1) * depth
        hi, lo = [
            jnp.concatenate([buf[first : first + padded, :], buf[second : second + padded, :]], axis=1)
            for buf in (cost_hi, cost_lo)
        ]
        y = dot3(vol_2[...], m, hi, lo)
        for h in range(2):
            z = taps(y[:, h * cols : (h + 1) * cols], m // 3, lane)
            out[pl.ds(d + h, m // 3, stride=DISP), :] = z

    correlate(range(CHUNK + 2))
    for d in range(0, DISP, CHUNK):
        correlate(range(d + CHUNK + 2, min(d + 2 * CHUNK + 2, DISP)))
        for e in range(d, d + CHUNK, 2):
            filtered(e)


def on_device(images, conv_weight, lift_weight, vol_weight):
    rows, cin, cols = images.shape
    outc, groups = vol_weight.shape[3:]
    feat = lift_weight.shape[0]
    per = feat // groups
    depth = (rows + 2) * groups
    padded = -(-3 * depth // 256) * 256
    m = 3 * rows * outc
    length = DISP * depth + padded
    vmem = pl.BlockSpec(memory_space=pltpu.VMEM)
    edge = pltpu.VMEM((2, cin, cols), f32)
    first_a, first_b, vol_2 = pl.pallas_call(
        gather,
        out_shape=[
            jax.ShapeDtypeStruct((per, depth, cols), f32),
            jax.ShapeDtypeStruct((per, depth, cols), f32),
            jax.ShapeDtypeStruct((2 * m, padded), bf16),
        ],
        in_specs=[vmem] * 4,
        out_specs=[vmem] * 3,
        scratch_shapes=[
            edge,
            edge,
            pltpu.VMEM((rows, cin, cols), f32),
            edge,
            edge,
            pltpu.VMEM((m, padded), f32),
            pltpu.VMEM((6 * cin, 3 * cin), bf16),
            pltpu.VMEM((2 * feat, cin), bf16),
            pltpu.SemaphoreType.DMA((5,)),
            pltpu.SemaphoreType.DMA((5,)),
        ],
        compiler_params=pltpu.CompilerParams(
            vmem_limit_bytes=32 << 20, collective_id=0, has_side_effects=True
        ),
    )(images, conv_weight, lift_weight, vol_weight)
    flat = pl.pallas_call(
        compute,
        out_shape=jax.ShapeDtypeStruct((rows * outc * DISP, cols), f32),
        in_specs=[vmem] * 3,
        out_specs=vmem,
        scratch_shapes=[
            pltpu.VMEM((-(-DISP // STEP), per, depth, cols), f32),
            pltpu.VMEM((STEP, per, depth, cols), f32),
            pltpu.VMEM((length, cols), bf16),
            pltpu.VMEM((length, cols), bf16),
        ],
        compiler_params=pltpu.CompilerParams(vmem_limit_bytes=32 << 20),
    )(first_a, first_b, vol_2)
    return flat.reshape(rows, outc, DISP, cols)


def solution(mesh):
    placed = (P(("scenes", "rows"), None, None), P(), P(), P())
    return jax.shard_map(
        on_device,
        mesh=mesh,
        in_specs=placed,
        out_specs=P(("scenes", "rows"), None, None, None),
        check_vma=False,
    )
```

```python
import jax
import jax.numpy as jnp
from jax import lax
from jax.experimental import pallas as pl
from jax.experimental.pallas import tpu as pltpu
from jax.sharding import PartitionSpec as P

DISP = 48
CHUNK = 4
STEP = 8
MESH = pl.DeviceIdType.MESH
f32, bf16 = jnp.float32, jnp.bfloat16


def split(x):
    hi = x.astype(bf16)
    return hi, (x - hi.astype(f32)).astype(bf16)


def dot(a, b):
    return jnp.dot(a, b, preferred_element_type=f32)


def dot3(stacked, rows, hi, lo):
    both = dot(stacked, hi)
    return both[:rows] + both[rows:] + dot(stacked[:rows], lo)


def taps(y, size, lane):
    cols = y.shape[1]
    before = jnp.where(lane >= 1, pltpu.roll(y[:size], 1, 1), 0.0)
    after = jnp.where(lane < cols - 1, pltpu.roll(y[2 * size :], cols - 1, 1), 0.0)
    return y[size : 2 * size] + before + after


def turned(x, by, is_right):
    cols = x.shape[-1]
    cut = by % cols
    return x if cut == 0 else pltpu.roll(x, jnp.where(is_right, cols - cut, cut), 1)


def place_of():
    position = lax.axis_index("rows")
    quarter = lax.axis_size("rows") // 4
    starts = (position == quarter) | (position == 3 * quarter)
    ends = (position == quarter - 1) | (position == 3 * quarter - 1)
    is_right = (position < quarter) | (position >= 3 * quarter)
    return starts, ends, is_right


def gather(
    images, cw_far, lw_far, vw_far, feat_a, feat_b, vol_2,
    before, after, there, there_before, there_after, vol_f, conv_2, lift_2,
    here, cw, lw, vw, send, recv, load,
):
    me, size = lax.axis_index("rows"), lax.axis_size("rows")
    up, down, partner = [lax.rem(me + by, size) for by in (1, size - 1, size // 2)]
    starts, ends, is_right = place_of()
    half = size // 2
    rows, cin, cols = images.shape
    halo = rows + 2
    feat = lw.shape[0]
    outc, groups = vw.shape[3:]
    per = feat // groups
    depth = halo * groups
    lane = lax.broadcasted_iota(jnp.int32, (1, cols), 1)

    to_first, to_last = me == half - 1, me == half
    from_first, from_last = me == 0, me == size - 1
    mated = to_first | to_last | from_first | from_last
    mate = jnp.where(to_first, 0, jnp.where(to_last, size - 1, jnp.where(from_first, half - 1, half)))

    fills = [(vw_far, vw), (cw_far, cw), (lw_far, lw), (images, here)]
    fills = [pltpu.make_async_copy(x, y, load.at[n]) for n, (x, y) in enumerate(fills)]
    for one in fills:
        one.start()

    barrier = pltpu.get_barrier_semaphore()

    @pl.when(mated)
    def _():
        pl.semaphore_signal(barrier, inc=1, device_id={"rows": mate}, device_id_type=MESH)

    for to in (up, down, partner):
        pl.semaphore_signal(barrier, inc=1, device_id={"rows": to}, device_id_type=MESH)
    @pl.when(mated)
    def _():
        pl.semaphore_wait(barrier, 4)

    @pl.when(jnp.logical_not(mated))
    def _():
        pl.semaphore_wait(barrier, 3)

    def copy(n, source, target, to, out=None):
        return pltpu.make_async_remote_copy(
            src_ref=source,
            dst_ref=target,
            send_sem=send.at[n if out is None else out],
            recv_sem=recv.at[n],
            device_id={"rows": to},
            device_id_type=MESH,
        )

    last, first = pl.ds(rows - 2, 2), pl.ds(0, 2)
    across = copy(0, images, there, partner)
    near = [copy(1, images.at[last], before, up), copy(2, images.at[first], after, down)]
    relays = [copy(3, there.at[last], there_before, up), copy(4, there.at[first], there_after, down)]
    direct = [
        copy(3, images.at[last], there_before, 0, 5),
        copy(4, images.at[first], there_after, size - 1, 6),
    ]
    across.start()

    @pl.when(to_first)
    def _():
        direct[0].start()

    @pl.when(to_last)
    def _():
        direct[1].start()

    for one in near:
        one.start()

    for one in fills:
        one.wait()

    vol_f[...] = jnp.zeros_like(vol_f)
    for dd in range(3):
        for dc in range(3):
            for r in range(rows):
                for dr in range(3):
                    top = (dc * rows + r) * outc
                    left = dd * depth + (r + dr) * groups
                    vol_f[top : top + outc, left : left + groups] = vw[dr, dd, dc] * (1.0 / per)
    m = 3 * rows * outc
    vol_2[:m], vol_2[m:] = split(vol_f[...])
    wide = jnp.concatenate([cw[dr].reshape(3 * cin, cin) for dr in range(3)], axis=1)
    conv_2[: 3 * cin], conv_2[3 * cin :] = split(wide)
    lift = jnp.concatenate([lw[pl.ds(k, groups, stride=per), :] for k in range(per)], axis=0)
    lift_2[:feat], lift_2[feat:] = split(lift)

    def features(above, middle, below, result, cut):
        parts = []
        for s in range(rows + 4):
            if s < 2:
                x = jnp.where(starts, 0.0, above[s])
            elif s < rows + 2:
                x = middle[s - 2]
            else:
                x = jnp.where(ends, 0.0, below[s - 2 - rows])
            parts.append(split(x))
        for r in range(0, halo, 2):
            pair = (r, min(r + 1, halo - 1))
            hi, lo = [
                jnp.concatenate(
                    [jnp.concatenate([parts[t + k][i] for k in range(3)], axis=0) for t in pair], axis=1
                )
                for i in range(2)
            ]
            y = dot3(conv_2[...], 3 * cin, hi, lo)
            hidden = []
            for n, t in enumerate(pair):
                h = jnp.maximum(taps(y[:, n * cols : (n + 1) * cols], cin, lane), 0.0)
                if cut and t == 0:
                    h = jnp.where(starts, 0.0, h)
                if cut and t == halo - 1:
                    h = jnp.where(ends, 0.0, h)
                hidden.append(h)
            f = dot3(lift_2[...], feat, *split(jnp.concatenate(hidden, axis=1)))
            for n, t in enumerate(pair):
                for k in range(per):
                    part = f[k * groups : (k + 1) * groups, n * cols : (n + 1) * cols]
                    result[k, t * groups : (t + 1) * groups, :] = part

    across.wait_recv()

    @pl.when(jnp.logical_not(from_last))
    def _():
        relays[0].start()

    @pl.when(jnp.logical_not(from_first))
    def _():
        relays[1].start()

    for one in near:
        one.wait_recv()
    features(before, here, after, feat_a.at[0], True)
    for b in range(1, STEP):
        for k in range(per):
            feat_a[b, k] = turned(feat_a[0, k], -b, is_right)
    for one in relays:
        one.wait_recv()
    features(there_before, there, there_after, feat_b, False)
    for one in (across, *near):
        one.wait_send()

    @pl.when(jnp.logical_not(from_last))
    def _():
        relays[0].wait_send()

    @pl.when(jnp.logical_not(from_first))
    def _():
        relays[1].wait_send()

    @pl.when(to_first)
    def _():
        direct[0].wait_send()

    @pl.when(to_last)
    def _():
        direct[1].wait_send()


def compute(feat_a, first_b, vol_2, out, feat_b, cost_hi, cost_lo):
    _, _, is_right = place_of()
    per, depth, cols = first_b.shape
    m, padded = vol_2.shape
    m = m // 2
    lane = lax.broadcasted_iota(jnp.int32, (1, cols), 1)

    for buf in (cost_hi, cost_lo):
        buf[:depth] = jnp.zeros((depth, cols), bf16)
        tail = buf.shape[0] - (DISP + 1) * depth
        buf[(DISP + 1) * depth :] = jnp.zeros((tail, cols), bf16)
    reach = jnp.where(is_right, cols - 1 - lane, lane)

    def correlate(disparities):
        for base in range(0, depth, 16):
            at = slice(base, base + 16)
            for d in disparities:
                step, b = divmod(d, STEP)
                total = None
                for k in range(per):
                    if b == 0 and step > 0:
                        feat_b[step, k, at, :] = turned(first_b[k, at, :], STEP * step, is_right)
                    right = feat_b[step, k, at, :] if step else first_b[k, at, :]
                    term = feat_a[b, k, at, :] * right
                    total = term if total is None else total + term
                hi, lo = split(jnp.where(reach >= d, turned(total, b, is_right), 0.0))
                place = (d + 1) * depth + base
                cost_hi[place : place + 16, :] = hi
                cost_lo[place : place + 16, :] = lo

    def filtered(d):
        first, second = d * depth, (d + 1) * depth
        hi, lo = [
            jnp.concatenate([buf[first : first + padded, :], buf[second : second + padded, :]], axis=1)
            for buf in (cost_hi, cost_lo)
        ]
        y = dot3(vol_2[...], m, hi, lo)
        for h in range(2):
            z = taps(y[:, h * cols : (h + 1) * cols], m // 3, lane)
            out[pl.ds(d + h, m // 3, stride=DISP), :] = z

    correlate(range(CHUNK + 2))
    for d in range(0, DISP, CHUNK):
        correlate(range(d + CHUNK + 2, min(d + 2 * CHUNK + 2, DISP)))
        for e in range(d, d + CHUNK, 2):
            filtered(e)


def on_device(images, conv_weight, lift_weight, vol_weight):
    rows, cin, cols = images.shape
    outc, groups = vol_weight.shape[3:]
    feat = lift_weight.shape[0]
    per = feat // groups
    depth = (rows + 2) * groups
    padded = -(-3 * depth // 256) * 256
    m = 3 * rows * outc
    length = DISP * depth + padded
    vmem = pl.BlockSpec(memory_space=pltpu.VMEM)
    edge = pltpu.VMEM((2, cin, cols), f32)
    first_a, first_b, vol_2 = pl.pallas_call(
        gather,
        out_shape=[
            jax.ShapeDtypeStruct((STEP, per, depth, cols), f32),
            jax.ShapeDtypeStruct((per, depth, cols), f32),
            jax.ShapeDtypeStruct((2 * m, padded), bf16),
        ],
        in_specs=[pl.BlockSpec(memory_space=pltpu.HBM)] * 4,
        out_specs=[vmem] * 3,
        scratch_shapes=[
            edge,
            edge,
            pltpu.VMEM((rows, cin, cols), f32),
            edge,
            edge,
            pltpu.VMEM((m, padded), f32),
            pltpu.VMEM((6 * cin, 3 * cin), bf16),
            pltpu.VMEM((2 * feat, cin), bf16),
            pltpu.VMEM(images.shape, f32),
            pltpu.VMEM(conv_weight.shape, f32),
            pltpu.VMEM(lift_weight.shape, f32),
            pltpu.VMEM(vol_weight.shape, f32),
            pltpu.SemaphoreType.DMA((7,)),
            pltpu.SemaphoreType.DMA((5,)),
            pltpu.SemaphoreType.DMA((4,)),
        ],
        compiler_params=pltpu.CompilerParams(
            vmem_limit_bytes=32 << 20, collective_id=0, has_side_effects=True
        ),
    )(images, conv_weight, lift_weight, vol_weight)
    flat = pl.pallas_call(
        compute,
        out_shape=jax.ShapeDtypeStruct((rows * outc * DISP, cols), f32),
        in_specs=[vmem] * 3,
        out_specs=vmem,
        scratch_shapes=[
            pltpu.VMEM((-(-DISP // STEP), per, depth, cols), f32),
            pltpu.VMEM((length, cols), bf16),
            pltpu.VMEM((length, cols), bf16),
        ],
        compiler_params=pltpu.CompilerParams(vmem_limit_bytes=32 << 20),
    )(first_a, first_b, vol_2)
    return flat.reshape(rows, outc, DISP, cols)


def solution(mesh):
    placed = (P(("scenes", "rows"), None, None), P(), P(), P())
    return jax.shard_map(
        on_device,
        mesh=mesh,
        in_specs=placed,
        out_specs=P(("scenes", "rows"), None, None, None),
        check_vma=False,
    )
```
